32 devices in a mesh: lon: 4 (over x, core), lat: 2 (over y), frame: 4 (over z).
Axes of the slice: x: 2, y: 2, z: 4, core: 2. Of those that a mesh axis runs over, the one named last changes fastest.
Arguments:
- features: bfloat16 [4, 128, 64, 256], P('frame', 'lon', 'lat'), may hold values from -6 to 6
- cotangent: bfloat16 [4, 128, 64, 162], P('frame', 'lon', 'lat'), may hold values from -6 to 6
Outputs:
- grads: bfloat16 [4, 128, 64, 256], P('frame', 'lon', 'lat')
The draws below stay inside these ranges and needn't reach their ends.
All inputs are finite; a program needn't handle non-finite values.
Results may differ from the reference program's by a relative error of at most 0.0023.
Values may be sent and summed in bfloat16 or wider, within the bound.
A program may use at most 64 MiB of HBM per device.

```python
import jax
import jax.numpy as jnp
import numpy as np
from jax import lax

CHANNELS = 256
LEVELS = 2
RAD = 4
LON_DEV = 32
LAT_DEV = 32
RIM = 8
FRAMES = 4
NLON = 128
NLAT = 64
N_LON = 4
N_LAT = 2


def levels(rng, shape, shards, least, high):
    def one(dim, blocks):
        draws = jax.random.uniform(jax.random.fold_in(jax.random.fold_in(rng, 6), dim), (blocks,), jnp.float32, least / len(shards), high / len(shards))
        return jnp.repeat(jnp.exp(draws), shape[dim] // blocks).reshape((-1,) + (1,) * (len(shape) - dim - 1))

    loudness = one(*shards[0])
    for cut in shards[1:]:
        loudness = loudness * one(*cut)
    return loudness


def centred(own_key, dims, scale, bound, cuts=(), held_as=jnp.bfloat16):
    entries = scale * jax.random.normal(own_key, dims, jnp.float32)
    if cuts:
        entries = entries * levels(own_key, dims, cuts, -0.22, 0.18)
    return jnp.clip(entries, -bound, bound).astype(held_as)


def setup_inputs(seed: int = 0) -> dict:
    splits = jax.random.split(jax.random.key(seed), 3)
    return {
        "features": centred(splits[0], (FRAMES, NLON, NLAT, CHANNELS), 1.0, 6.0, ((0, 4), (1, 4), (2, 2))),
        "cotangent": centred(splits[1], (FRAMES, NLON, NLAT, LEVELS * (2 * RAD + 1) * (2 * RAD + 1)), 1.0, 6.0, ((0, 4), (1, 4), (2, 2))),
    }


def pooled(extended, factor):
    if factor == 1:
        return extended
    count_x, count_y, channels = extended.shape
    grouped = extended.astype(jnp.float32).reshape(count_x // factor, factor, count_y // factor, factor, channels)
    return (lax.optimization_barrier(jnp.sum(grouped, axis=(1, 3))) / (factor * factor)).astype(jnp.bfloat16)

def query_grad(cot_tile, next_ext):
    tile_cols, tile_rows = (cot_tile.shape[0], cot_tile.shape[1])
    across = 2 * RAD + 1
    stride = 4
    summed = jnp.zeros((tile_cols, tile_rows, next_ext.shape[2]), jnp.float32)
    for pyramid_level in range(LEVELS):
        factor = 2 ** pyramid_level
        anchor = RIM // factor - RAD
        key_rows = tile_rows // factor + 2 * RAD
        key_map = pooled(next_ext, factor)[:, anchor:anchor + key_rows]
        selector = jnp.asarray((np.arange(key_rows)[None, :, None] == (np.arange(tile_rows) // factor)[:, None, None] + np.arange(across)[None, None, :]).astype(np.float32))
        first_chan = pyramid_level * across * across

        def one_block(position):
            start_col = position * stride
            key_block = lax.dynamic_slice_in_dim(key_map, (start_col // factor + anchor).astype(jnp.int32), stride // factor + 2 * RAD, 0)
            window = jnp.stack([jnp.repeat(key_block[shift_col:shift_col + stride // factor], factor, axis=0) for shift_col in range(across)], axis=1)
            window = window.reshape(stride, across * key_rows, window.shape[3]).astype(jnp.float32)
            cot_block = lax.dynamic_slice_in_dim(cot_tile, start_col.astype(jnp.int32), stride, 0)
            portion = cot_block[:, :, first_chan:first_chan + across * across].reshape(stride, tile_rows, across, across).astype(jnp.float32)
            banded = jnp.einsum('xyad,yrd->xyar', portion, selector.astype(jnp.float32))
            banded = banded.reshape(stride, tile_rows, across * key_rows)
            return jnp.einsum('xyk,xkc->xyc', banded, window)
        gradient = lax.map(one_block, jnp.arange(tile_cols // stride, dtype=jnp.int32))
        summed = summed + gradient.reshape(tile_cols, tile_rows, -1)
    return summed * next_ext.shape[2] ** (-0.5)

def key_grad(query_ext, cot_ext):
    tile_cols = query_ext.shape[0] - 2 * RIM
    tile_rows = query_ext.shape[1] - 2 * RIM
    across = 2 * RAD + 1
    summed = jnp.zeros((tile_cols, tile_rows, query_ext.shape[2]), jnp.float32)
    for pyramid_level in range(LEVELS):
        factor = 2 ** pyramid_level
        anchor = RIM - RAD * factor
        row_count = tile_rows + 2 * RAD * factor
        key_cols = tile_cols // factor
        key_rows = tile_rows // factor
        stride = max(1, 4 // factor)
        reach = across * factor
        selector = jnp.asarray((np.arange(key_rows)[:, None, None] == (np.arange(row_count) // factor)[None, :, None] + np.arange(across)[None, None, :] - 2 * RAD).astype(np.float32))
        first_chan = pyramid_level * across * across
        feat_rows = query_ext[:, anchor:anchor + row_count]
        cot_rows = cot_ext[:, anchor:anchor + row_count, first_chan:first_chan + across * across].reshape(cot_ext.shape[0], row_count, across, across)

        def one_block(position):
            start_col = (position * stride * factor + anchor).astype(jnp.int32)
            extent = factor * (stride + 2 * RAD)
            feat_block = lax.dynamic_slice_in_dim(feat_rows, start_col, extent, 0)
            cot_block = lax.dynamic_slice_in_dim(cot_rows, start_col, extent, 0)
            window = jnp.stack([feat_block[shift_col:shift_col + factor * stride:factor] for shift_col in range(reach)], axis=1)
            window = window.reshape(stride, reach * row_count, window.shape[3]).astype(jnp.float32)
            portion = jnp.stack([cot_block[shift_col:shift_col + factor * stride:factor, :, 2 * RAD - shift_col // factor] for shift_col in range(reach)], axis=1).astype(jnp.float32)
            banded = jnp.einsum('ujyd,vyd->uvjy', portion, selector.astype(jnp.float32))
            banded = banded.reshape(stride, key_rows, reach * row_count)
            return jnp.einsum('uvk,ukc->uvc', banded, window)
        gradient = lax.map(one_block, jnp.arange(key_cols // stride, dtype=jnp.int32)).reshape(key_cols, key_rows, -1)
        gradient = jnp.repeat(jnp.repeat(gradient, factor, axis=0), factor, axis=1)
        summed = summed + gradient / (factor * factor)
    return summed * query_ext.shape[2] ** (-0.5)

def extend_global(field):
    wrapped = jnp.concatenate([field[-RIM:], field, field[:RIM]], axis=0)
    return jnp.pad(wrapped, ((0, 0), (RIM, RIM), (0, 0)))

def over_tiles(kernel, extended):

    def one_tile(position):
        lon_pos = position // N_LAT
        lat_pos = position % N_LAT
        pieces = tuple((lax.dynamic_slice(item, (lon_pos * LON_DEV, lat_pos * LAT_DEV, jnp.int32(0)), (LON_DEV + 2 * RIM, LAT_DEV + 2 * RIM, item.shape[2])) for item in extended))
        return kernel(pieces)
    tiles_out = lax.map(one_tile, jnp.arange(N_LON * N_LAT, dtype=jnp.int32))
    tiles_out = tiles_out.reshape(N_LON, N_LAT, LON_DEV, LAT_DEV, -1)
    return tiles_out.transpose(0, 2, 1, 3, 4).reshape(N_LON * LON_DEV, N_LAT * LAT_DEV, -1)

def reference(features, cotangent):
    frame_count = features.shape[0]
    carried = jnp.zeros(features.shape[1:], jnp.float32)
    outputs = []
    for frame_pos in range(frame_count):
        if frame_pos + 1 < frame_count:
            next_ext = extend_global(features[frame_pos + 1])
            query_ext = extend_global(features[frame_pos])
            cot_ext = extend_global(cotangent[frame_pos])
            own_grad = over_tiles(lambda pieces: query_grad(pieces[1][RIM:RIM + LON_DEV, RIM:RIM + LAT_DEV], pieces[0]), (next_ext, cot_ext))
            following = over_tiles(lambda pieces: key_grad(pieces[0], pieces[1]), (query_ext, cot_ext))
        else:
            own_grad = jnp.zeros(features.shape[1:], jnp.float32)
            following = jnp.zeros(features.shape[1:], jnp.float32)
        outputs.append((own_grad + carried).astype(jnp.bfloat16))
        carried = following
    return jnp.stack(outputs, axis=0)
```

```python
import jax
import jax.numpy as jnp
import numpy as np
from jax import lax
from jax.experimental import pallas as pl
from jax.experimental.pallas import tpu as pltpu
from jax.sharding import PartitionSpec as P

LEVELS = 2
RAD = 4
RIM = 8
ACROSS = 2 * RAD + 1
HALF = 512


def extended_2(array, sides, width, wrap):
    for axis, dim in sides:
        size, length = (lax.axis_size(axis), array.shape[dim])
        up = [(i, (i + 1) % size) for i in range(size if wrap else size - 1)]
        down = [(j, i) for i, j in up]
        last = lax.slice_in_dim(array, length - width, length, axis=dim)
        first = lax.slice_in_dim(array, 0, width, axis=dim)
        before = lax.ppermute(last, axis, up)
        after = lax.ppermute(first, axis, down)
        array = jnp.concatenate([before, array, after], axis=dim)
    return array


def from_behind(value, axis, steps):
    count = lax.axis_size(axis)
    first, last = (max(0, -steps), min(count, count - steps))
    return lax.ppermute(value, axis, [(source, source + steps) for source in range(first, last)])


def spreader(rows):
    out = np.zeros((LEVELS * ACROSS * ACROSS, LEVELS * HALF), np.float32)
    for a in range(ACROSS):
        for b in range(ACROSS):
            out[a * ACROSS + b, a * rows + RAD + b] = 1
            out[ACROSS * ACROSS + a * ACROSS + b, HALF + a * rows + 2 * b] = 1
    return jnp.asarray(out).astype(jnp.bfloat16)


def sheared(spread):
    return pltpu.roll(spread, 0, 1, stride=1, stride_axis=0).astype(jnp.bfloat16)


def pair_sum(value):
    rows = value.shape[0]
    odd = lax.broadcasted_iota(jnp.int32, value.shape, 0) % 2 == 1
    return value + jnp.where(odd, pltpu.roll(value, 1, 0), pltpu.roll(value, rows - 1, 0))


def own_kernel(cot_ref, ext_ref, spread_ref, out_ref, pool_ref):
    cols, rows, chans = out_ref.shape
    wide = rows + 2 * RIM
    depth = ACROSS * wide

    @pl.loop(0, (cols + 2 * RIM) // 2)
    def _(pos):
        both = ext_ref[2 * pos].astype(jnp.float32) + ext_ref[2 * pos + 1].astype(jnp.float32)
        pool_ref[pos] = (pair_sum(both) * 0.25).astype(jnp.bfloat16)

    @pl.loop(0, cols)
    def _(x):
        spread = jnp.dot(cot_ref[x], spread_ref[...], preferred_element_type=jnp.float32)
        near = sheared(spread[:, :HALF])[:, :depth]
        far = sheared(spread[:, HALF:])[:, :depth]
        keys = ext_ref[pl.ds(x + RAD, ACROSS)].reshape(depth, chans)
        pooled = pool_ref[pl.ds(x // 2, ACROSS)].reshape(depth, chans)
        total = jnp.dot(near, keys, preferred_element_type=jnp.float32)
        total = total + jnp.dot(far, pooled, preferred_element_type=jnp.float32)
        out_ref[x] = total * chans ** (-0.5)


def back_kernel(ext_ref, spread_ref, out_ref, near_ref, far_ref):
    cols, rows, chans = out_ref.shape
    wide = rows + 2 * RIM
    contract = (((0,), (0,)), ((), ()))

    @pl.loop(0, cols + 4 * RIM)
    def _(pos):
        near_ref[pos] = jnp.zeros((rows, chans), jnp.float32)
        far_ref[pos] = jnp.zeros((rows, chans), jnp.float32)

    @pl.loop(0, cols + 2 * RIM)
    def _(x):
        feats = ext_ref[x, :, :chans]
        spread = jnp.dot(ext_ref[x, :, chans:], spread_ref[...], preferred_element_type=jnp.float32)
        near = lax.dot_general(sheared(spread[:, :HALF]), feats, contract, preferred_element_type=jnp.float32)
        far = lax.dot_general(sheared(spread[:, HALF:]), feats, contract, preferred_element_type=jnp.float32)
        for a in range(ACROSS):
            begin = a * wide + 2 * RIM
            near_ref[x + a + RAD] += near[begin : begin + rows]
            far_ref[x + 2 * a] += far[begin : begin + rows]

    @pl.loop(0, cols // 2)
    def _(pos):
        u = 2 * pos + 2 * RIM
        both = pair_sum(far_ref[u] + far_ref[u + 1]) * 0.25
        out_ref[2 * pos] = (near_ref[u] + both) * chans ** (-0.5)
        out_ref[2 * pos + 1] = (near_ref[u + 1] + both) * chans ** (-0.5)


def local_call(kernel, cols, rows, chans, scratch, flops, *args):
    vmem = pl.BlockSpec(memory_space=pltpu.VMEM)
    return pl.pallas_call(
        kernel,
        out_shape=jax.ShapeDtypeStruct((cols, rows, chans), jnp.float32),
        in_specs=[vmem] * len(args),
        out_specs=vmem,
        scratch_shapes=scratch,
        cost_estimate=pl.CostEstimate(flops=flops, bytes_accessed=4 << 20, transcendentals=0),
        compiler_params=pltpu.CompilerParams(vmem_limit_bytes=40 << 20),
    )(*args)


def extend(stacked):
    beside_all = extended_2(stacked, (("lon", 0),), RIM, True)
    return extended_2(beside_all, (("lat", 1),), RIM, False)


def body(features, cotangent):
    _, cols, rows, chans = features.shape
    wide = rows + 2 * RIM
    spread = spreader(wide)
    following = from_behind(features, "frame", -1)
    query_ext = extend(jnp.concatenate([features[0], cotangent[0]], axis=2))
    next_ext = extend(following[0])
    wider = pltpu.VMEM((cols + 4 * RIM, rows, chans), jnp.float32)
    key_part = local_call(back_kernel, cols, rows, chans, [wider, wider], 10**10, query_ext, spread)
    carried = from_behind(key_part, "frame", 1)
    pool = pltpu.VMEM((cols // 2 + RIM, wide, chans), jnp.bfloat16)
    own = local_call(own_kernel, cols, rows, chans, [pool], 10**10, cotangent[0], next_ext, spread)
    return (own + carried).astype(jnp.bfloat16)[None]


def solution(mesh):
    placed = (P("frame", "lon", "lat", None), P("frame", "lon", "lat", None))
    return jax.shard_map(
        body, mesh=mesh, in_specs=placed, out_specs=P("frame", "lon", "lat", None), check_vma=False
    )
```

```python
import jax
import jax.numpy as jnp
import numpy as np
from jax import lax
from jax.experimental import pallas as pl
from jax.experimental.pallas import tpu as pltpu
from jax.sharding import PartitionSpec as P

LEVELS = 2
RAD = 4
RIM = 8
ACROSS = 2 * RAD + 1
BLOCK = 4


def extended(array, axis, dim, wrap):
    size, length = (lax.axis_size(axis), array.shape[dim])
    last = lax.slice_in_dim(array, length - RIM, length, axis=dim)
    first = lax.slice_in_dim(array, 0, RIM, axis=dim)
    if size == 2 and not wrap:
        lower = lax.axis_index(axis) == 0
        met = lax.ppermute(jnp.where(lower, last, first), axis, [(0, 1), (1, 0)])
        none = jnp.zeros_like(met)
        before, after = jnp.where(lower, none, met), jnp.where(lower, met, none)
    else:
        up = [(i, (i + 1) % size) for i in range(size if wrap else size - 1)]
        before = lax.ppermute(last, axis, up)
        after = lax.ppermute(first, axis, [(j, i) for i, j in up])
    return jnp.concatenate([before, array, after], axis=dim)


def from_behind(value, axis, steps):
    count = lax.axis_size(axis)
    first, last = (max(0, -steps), min(count, count - steps))
    return lax.ppermute(value, axis, [(source, source + steps) for source in range(first, last)])


def spreader(rows, starts, lanes):
    out = np.zeros((LEVELS * ACROSS * ACROSS, sum(lanes)), np.float32)
    for a in range(ACROSS):
        for b in range(ACROSS):
            out[a * ACROSS + b, a * starts[0] * rows + RAD + b] = 1
            out[ACROSS * ACROSS + a * ACROSS + b, lanes[0] + a * starts[1] * rows + 2 * b] = 1
    return jnp.asarray(out).astype(jnp.bfloat16)


def sheared(spread, rows, shifts):
    parts = [
        pltpu.roll(spread[i * rows : (i + 1) * rows], shift, 1, stride=1, stride_axis=0)
        for i, shift in enumerate(shifts)
    ]
    return jnp.concatenate(parts, axis=0).astype(jnp.bfloat16)


def pair_sum(value):
    rows = value.shape[0]
    odd = lax.broadcasted_iota(jnp.int32, value.shape, 0) % 2 == 1
    return value + jnp.where(odd, pltpu.roll(value, 1, 0), pltpu.roll(value, rows - 1, 0))


def padded(lanes):
    return -(-lanes // 128) * 128


def own_lanes(wide):
    return padded((ACROSS + BLOCK - 1) * wide), padded((ACROSS + BLOCK // 2 - 1) * wide)


def back_lanes(wide):
    return padded((ACROSS + BLOCK - 1) * wide), padded((2 * ACROSS + BLOCK - 2) * wide)


def own_kernel(cot_ref, ext_ref, spread_ref, out_ref, pool_ref):
    cols, rows, chans = out_ref.shape
    wide = rows + 2 * RIM
    lanes = own_lanes(wide)
    near_cols, far_cols = ACROSS + BLOCK - 1, ACROSS + BLOCK // 2 - 1

    @pl.loop(0, (cols + 2 * RIM) // 2)
    def _(pos):
        both = ext_ref[2 * pos].astype(jnp.float32) + ext_ref[2 * pos + 1].astype(jnp.float32)
        pool_ref[pos] = (pair_sum(both) * 0.25).astype(jnp.bfloat16)

    @pl.loop(0, cols // BLOCK)
    def _(pos):
        x = pos * BLOCK
        cot = cot_ref[pl.ds(x, BLOCK)].reshape(BLOCK * rows, cot_ref.shape[2])
        spread = jnp.dot(cot, spread_ref[...], preferred_element_type=jnp.float32)
        near = sheared(spread[:, : lanes[0]], rows, [i * wide for i in range(BLOCK)])
        far = sheared(spread[:, lanes[0] :], rows, [i // 2 * wide for i in range(BLOCK)])
        keys = ext_ref[pl.ds(x + RAD, near_cols)].reshape(near_cols * wide, chans)
        pooled = pool_ref[pl.ds(pos * (BLOCK // 2), far_cols)].reshape(far_cols * wide, chans)
        total = jnp.dot(near[:, : near_cols * wide], keys, preferred_element_type=jnp.float32)
        total = total + jnp.dot(far[:, : far_cols * wide], pooled, preferred_element_type=jnp.float32)
        out_ref[pl.ds(x, BLOCK)] = (total * chans ** (-0.5)).reshape(BLOCK, rows, chans)


def back_kernel(ext_ref, spread_ref, out_ref, near_ref, far_ref):
    cols, rows, chans = out_ref.shape
    wide = rows + 2 * RIM
    lanes = back_lanes(wide)
    contract = (((0,), (0,)), ((), ()))

    @pl.loop(0, cols + 4 * RIM)
    def _(pos):
        near_ref[pos] = jnp.zeros((rows, chans), jnp.float32)
        far_ref[pos] = jnp.zeros((rows, chans), jnp.float32)

    @pl.loop(0, (cols + 2 * RIM) // BLOCK)
    def _(pos):
        x = pos * BLOCK
        feats = ext_ref[pl.ds(x, BLOCK), :, :chans].reshape(BLOCK * wide, chans)
        cot = ext_ref[pl.ds(x, BLOCK), :, chans:]
        cot = cot.reshape(BLOCK * wide, cot.shape[2])
        spread = jnp.dot(cot, spread_ref[...], preferred_element_type=jnp.float32)
        shifts = [i * wide for i in range(BLOCK)]
        near = sheared(spread[:, : lanes[0]], wide, shifts)
        far = sheared(spread[:, lanes[0] :], wide, shifts)
        near = lax.dot_general(near, feats, contract, preferred_element_type=jnp.float32)
        far = lax.dot_general(far, feats, contract, preferred_element_type=jnp.float32)
        for k in range(ACROSS + BLOCK - 1):
            begin = k * wide + 2 * RIM
            near_ref[x + k + RAD] += near[begin : begin + rows]
        for k in range(2 * ACROSS + BLOCK - 2):
            begin = k * wide + 2 * RIM
            far_ref[x + k] += far[begin : begin + rows]

    @pl.loop(0, cols // 2)
    def _(pos):
        u = 2 * pos + 2 * RIM
        both = pair_sum(far_ref[u] + far_ref[u + 1]) * 0.25
        out_ref[2 * pos] = (near_ref[u] + both) * chans ** (-0.5)
        out_ref[2 * pos + 1] = (near_ref[u + 1] + both) * chans ** (-0.5)


def local_call(kernel, cols, rows, chans, scratch, flops, *args):
    vmem = pl.BlockSpec(memory_space=pltpu.VMEM)
    return pl.pallas_call(
        kernel,
        out_shape=jax.ShapeDtypeStruct((cols, rows, chans), jnp.float32),
        in_specs=[vmem] * len(args),
        out_specs=vmem,
        scratch_shapes=scratch,
        cost_estimate=pl.CostEstimate(flops=flops, bytes_accessed=4 << 20, transcendentals=0),
        compiler_params=pltpu.CompilerParams(vmem_limit_bytes=40 << 20),
    )(*args)


def extend(stacked):
    return extended(extended(stacked, "lon", 0, True), "lat", 1, False)


def body(features, cotangent):
    _, cols, rows, chans = features.shape
    wide = rows + 2 * RIM
    back_spread = spreader(wide, (1, 2), back_lanes(wide))
    own_spread = spreader(wide, (1, 1), own_lanes(wide))
    following = from_behind(features, "frame", -1)
    query_ext = extend(jnp.concatenate([features[0], cotangent[0]], axis=2))
    next_ext = extend(following[0])
    wider = pltpu.VMEM((cols + 4 * RIM, rows, chans), jnp.float32)
    key_part = local_call(back_kernel, cols, rows, chans, [wider, wider], 10**10, query_ext, back_spread)
    carried = from_behind(key_part, "frame", 1)
    pool = pltpu.VMEM((cols // 2 + RIM, wide, chans), jnp.bfloat16)
    own = local_call(own_kernel, cols, rows, chans, [pool], 10**10, cotangent[0], next_ext, own_spread)
    return (own + carried).astype(jnp.bfloat16)[None]


def solution(mesh):
    placed = (P("frame", "lon", "lat", None), P("frame", "lon", "lat", None))
    return jax.shard_map(
        body, mesh=mesh, in_specs=placed, out_specs=P("frame", "lon", "lat", None), check_vma=False
    )
```
